32 devices in a mesh: frames: 8 (over y, x, core), pix: 4 (over z).
Axes of the slice: x: 2, y: 2, z: 4, core: 2. Of those that a mesh axis runs over, the one named last changes fastest.
Arguments:
- edge_frames: int32 [2, 1536], P(None, 'frames'), may hold values from 0 to 127, as said below
- rotvec: float32 [3, 128], replicated, may hold values from -0.06 to 0.06
- trans: float32 [3, 128], replicated, may hold values from -0.15 to 0.15
- inv_depth: float32 [128, 3072], P('frames', 'pix'), may hold values from 0.2 to 1
- depth_damping: float32 [128, 3072], P('frames', 'pix'), may hold values from 0.01 to 0.1
- flow: float32 [1536, 2, 3072], P('frames', None, 'pix'), may hold values from -0.3 to 0.3
- weight: float32 [1536, 2, 3072], P('frames', None, 'pix'), may hold values from 0.02 to 1
- mask: int32 [1536, 3072], P('frames', 'pix'), may hold values 0 or 1
Outputs:
- pose_step: float32 [6, 128], P(None, 'frames')
- depth_step: float32 [128, 3072], P('frames', 'pix')
The draws below stay inside these ranges and needn't reach their ends.
Inputs may be any that keep to these rules, and one draw needn't show every extreme that they name: Edge e of the block of 192 edges held by one index of frames has its target edge_frames[1, e] among that index's 16 keyframes; its source edge_frames[0, e] differs from the target by 1 to 8, and in every block some source lies exactly 8 away.
All inputs are finite; a program needn't handle non-finite values. No bound on the sum of `mask` on one device may be relied on, other than what follows from the above.
Results may differ from the reference program's by a relative error of at most 0.00015.
Values sent between devices are 32-bit elements; how exact they have to be, the bound alone decides.
A program may use at most 64 MiB of HBM per device.

```python
import math
import jax
import jax.numpy as jnp
from jax import lax

F_DEV = 16
EDGE_DEV = 192
ROWS = 48
COLS = 64
RADIUS = 8
ITERS = 6
FRAMES = 128
EDGES = 1536
PIX = 3072


def draw_edge_frames(key, part):
    keys = jax.random.split(jax.random.fold_in(key, 11), 4)
    index = jnp.arange(EDGES, dtype=jnp.int32)
    block = index // EDGE_DEV
    slot = index % EDGE_DEV
    first = jax.random.randint(keys[0], (EDGES,), 0, F_DEV)
    second = jax.random.randint(keys[1], (EDGES,), 0, F_DEV)
    local = jnp.minimum(first, second)
    local = jnp.where(slot == 0, 0, jnp.where(slot == 1, F_DEV - 1, local))
    offset = jax.random.randint(keys[2], (EDGES,), 1, RADIUS + 1)
    offset = jnp.where(slot < 2, RADIUS, offset)
    sign = 2 * jax.random.randint(keys[3], (EDGES,), 0, 2) - 1
    sign = jnp.where(slot == 0, -1, jnp.where(slot == 1, 1, sign))
    target = block * F_DEV + local
    source = target + sign * offset
    source = jnp.where((source < 0) | (source >= FRAMES), target - sign * offset, source)
    return jnp.stack([source, target]).astype(jnp.int32)


def draw_flow(key, part):
    keys = jax.random.split(jax.random.fold_in(key, 23), 2)
    shared = jnp.clip(0.06 * jax.random.normal(keys[0], (EDGES, 2, 1), jnp.float32), -0.2, 0.2)
    noise = jnp.clip(0.03 * jax.random.normal(keys[1], (EDGES, 2, PIX), jnp.float32), -0.1, 0.1)
    return shared + noise


def touch_ends(drawn, stream_key, low, high):
    place = [jax.random.randint(jax.random.fold_in(stream_key, axis), (), 0, length) for axis, length in enumerate(drawn.shape)]
    main_axis = drawn.shape.index(max(drawn.shape))
    neighbour = place[:main_axis] + [(place[main_axis] + 1) % drawn.shape[main_axis]] + place[main_axis + 1:]
    return drawn.at[tuple(place)].set(low).at[tuple(neighbour)].set(high)


def shard_levels(rng, shape, cuts, least, largest):
    gain = 1.0
    for axis_at, parts in cuts:
        steps = jax.random.uniform(jax.random.fold_in(jax.random.fold_in(rng, 6), axis_at), (parts,), jnp.float32, least / len(cuts), largest / len(cuts))
        gain = gain * jnp.repeat(jnp.exp(steps), shape[axis_at] // parts).reshape((-1,) + (1,) * (len(shape) - 1 - axis_at))
    return gain


def setup_inputs(seed: int = 0) -> dict:
    key_list = jax.random.split(jax.random.key(seed), 9)
    return {
        "edge_frames": draw_edge_frames(jax.random.fold_in(key_list[8], 71), 0),
        "rotvec": jnp.clip(jax.random.uniform(key_list[1], (3, FRAMES), jnp.float32, -0.06, 0.06), -0.06, 0.06),
        "trans": jnp.clip(jax.random.uniform(key_list[2], (3, FRAMES), jnp.float32, -0.15, 0.15), -0.15, 0.15),
        "inv_depth": jnp.clip(jnp.exp(math.log(1.0) - 1.609438 * jax.random.uniform(key_list[3], (FRAMES, PIX), jnp.float32) ** shard_levels(key_list[3], (FRAMES, PIX), ((0, 8), (1, 4)), -0.2, 0.2)), 0.2, 1.0),
        "depth_damping": jnp.clip(jnp.exp(math.log(0.1) - 2.3025851 * jax.random.uniform(key_list[4], (FRAMES, PIX), jnp.float32) ** shard_levels(key_list[4], (FRAMES, PIX), ((0, 8), (1, 4)), -0.2, 0.2)), 0.01, 0.1),
        "flow": draw_flow(jax.random.fold_in(key_list[8], 71), 0),
        "weight": jnp.clip(jnp.exp(math.log(1.0) - 3.912023 * jax.random.uniform(key_list[6], (EDGES, 2, PIX), jnp.float32) ** shard_levels(key_list[6], (EDGES, 2, PIX), ((0, 8), (2, 4)), -0.2, 0.2)), 0.02, 1.0),
        "mask": touch_ends((jax.random.randint(key_list[7], (EDGES, PIX), 0, 4) < 3).astype(jnp.int32), jax.random.fold_in(key_list[7], 1), 0, 1),
    }


exact = lax.Precision.HIGHEST
pose_regularizer = 100.0


def pixel_coords(pixel):
    row = pixel // COLS
    column = pixel % COLS
    col_coord = (column.astype(jnp.float32) - 0.5 * (COLS - 1)) / COLS
    row_coord = (row.astype(jnp.float32) - 0.5 * (ROWS - 1)) / COLS
    return col_coord, row_coord


def rotations(rotvec):
    omega_x, omega_y, omega_z = rotvec[0], rotvec[1], rotvec[2]
    zero = jnp.zeros_like(omega_x)
    cross = [[zero, -omega_z, omega_y], [omega_z, zero, -omega_x], [-omega_y, omega_x, zero]]
    theta_sq = omega_x * omega_x + omega_y * omega_y + omega_z * omega_z
    first_coef = 1.0 - theta_sq / 6.0 + theta_sq * theta_sq / 120.0
    second_coef = 0.5 - theta_sq / 24.0 + theta_sq * theta_sq / 720.0
    lines = []
    for row in range(3):
        entries = []
        for column in range(3):
            square = cross[row][0] * cross[0][column] + cross[row][1] * cross[1][column] + cross[row][2] * cross[2][column]
            entries.append(float(row == column) + first_coef * cross[row][column] + second_coef * square)
        lines.append(jnp.stack(entries))
    return jnp.stack(lines)


def relative(rot, trans, source, target):
    rot_source = jnp.take(rot, source, axis=2)
    rot_target = jnp.take(rot, target, axis=2)
    rel_rot = jnp.einsum('ike,jke->ije', rot_target, rot_source, precision=exact)
    rel_trans = jnp.take(trans, target, axis=1) - jnp.einsum('ije,je->ie', rel_rot, jnp.take(trans, source, axis=1), precision=exact)
    zero = jnp.zeros_like(rel_trans[0])
    skew = jnp.stack([jnp.stack([zero, -rel_trans[2], rel_trans[1]]),
                      jnp.stack([rel_trans[2], zero, -rel_trans[0]]),
                      jnp.stack([-rel_trans[1], rel_trans[0], zero])])
    corner = jnp.einsum('ike,kje->ije', skew, rel_rot, precision=exact)
    upper = jnp.concatenate([rel_rot, corner], axis=1)
    lower = jnp.concatenate([jnp.zeros_like(rel_rot), rel_rot], axis=1)
    return rel_rot, rel_trans, jnp.concatenate([upper, lower], axis=0)


def geometry(rel_rot, rel_trans, depth, flow, weight, mask, col_coord, row_coord):
    def coordinate(line):
        return (rel_rot[line, 0][:, None] * col_coord + rel_rot[line, 1][:, None] * row_coord
                + rel_rot[line, 2][:, None] + depth * rel_trans[line][:, None])
    inverse_z = 1.0 / coordinate(2)
    proj_u = coordinate(0) * inverse_z
    proj_v = coordinate(1) * inverse_z
    depth_scale = depth * inverse_z
    slope_u = inverse_z * (rel_trans[0][:, None] - proj_u * rel_trans[2][:, None])
    slope_v = inverse_z * (rel_trans[1][:, None] - proj_v * rel_trans[2][:, None])
    live = mask.astype(jnp.float32)
    conf_u = weight[:, 0] * live
    conf_v = weight[:, 1] * live
    error_u = col_coord + flow[:, 0] - proj_u
    error_v = row_coord + flow[:, 1] - proj_v
    return proj_u, proj_v, depth_scale, slope_u, slope_v, conf_u, conf_v, error_u, error_v


def apply_pose(geo, motion):
    proj_u, proj_v, depth_scale = geo[0], geo[1], geo[2]
    part = [motion[index][:, None] for index in range(6)]
    cross_uv = proj_u * proj_v
    lin_u = depth_scale * (part[0] - proj_u * part[2]) - cross_uv * part[3] + (1.0 + proj_u * proj_u) * part[4] - proj_v * part[5]
    lin_v = depth_scale * (part[1] - proj_v * part[2]) - (1.0 + proj_v * proj_v) * part[3] + cross_uv * part[4] + proj_u * part[5]
    return lin_u, lin_v


def pose_terms(geo, part_u, part_v):
    proj_u, proj_v, depth_scale = geo[0], geo[1], geo[2]
    heavy_u = geo[5] * part_u
    heavy_v = geo[6] * part_v
    cross_uv = proj_u * proj_v
    entries = [depth_scale * heavy_u, depth_scale * heavy_v,
               -depth_scale * (proj_u * heavy_u + proj_v * heavy_v),
               -cross_uv * heavy_u - (1.0 + proj_v * proj_v) * heavy_v,
               (1.0 + proj_u * proj_u) * heavy_u + cross_uv * heavy_v,
               -proj_v * heavy_u + proj_u * heavy_v]
    return jnp.stack([jnp.sum(entry, axis=1) for entry in entries])


def spread(motion, source, target, adjoint):
    return jnp.take(motion, target, axis=1) - jnp.einsum('jke,ke->je', adjoint, jnp.take(motion, source, axis=1), precision=exact)


def reference(edge_frames, rotvec, trans, inv_depth, depth_damping, flow, weight, mask):
    col_coord, row_coord = pixel_coords(jnp.arange(PIX, dtype=jnp.int32))
    rot = rotations(rotvec)
    blocks = EDGES // EDGE_DEV
    packed = (edge_frames[0].reshape(blocks, EDGE_DEV), edge_frames[1].reshape(blocks, EDGE_DEV),
              flow.reshape(blocks, EDGE_DEV, 2, PIX), weight.reshape(blocks, EDGE_DEV, 2, PIX),
              mask.reshape(blocks, EDGE_DEV, PIX))

    def sweep(update, init):
        def advance(carry, item):
            source, target, flow_block, weight_block, mask_block = item
            rel_rot, rel_trans, adjoint = relative(rot, trans, source, target)
            geo = geometry(rel_rot, rel_trans, jnp.take(inv_depth, source, axis=0), flow_block,
                           weight_block, mask_block, col_coord, row_coord)
            return update(carry, source, target, adjoint, geo), None
        return lax.scan(advance, init, packed)[0]

    def totals_update(carry, source, target, adjoint, geo):
        terms = jnp.stack([geo[5] * geo[3] * geo[3] + geo[6] * geo[4] * geo[4],
                           -(geo[3] * geo[5] * geo[7] + geo[4] * geo[6] * geo[8])])
        return carry.at[:, source].add(terms)

    totals = sweep(totals_update, jnp.zeros((2, FRAMES, PIX), jnp.float32))
    curvature = totals[0] + depth_damping
    base_step = totals[1] / curvature

    def pose_sweep(motion, image):
        def update(carry, source, target, adjoint, geo):
            at_source = jnp.take(image, source, axis=0)
            if motion is None:
                part_u = -geo[7] - geo[3] * at_source
                part_v = -geo[8] - geo[4] * at_source
            else:
                lin_u, lin_v = apply_pose(geo, spread(motion, source, target, adjoint))
                part_u = lin_u - geo[3] * at_source
                part_v = lin_v - geo[4] * at_source
            target_terms = pose_terms(geo, part_u, part_v)
            source_terms = -jnp.einsum('jke,je->ke', adjoint, target_terms, precision=exact)
            return carry.at[:, target].add(target_terms).at[:, source].add(source_terms)
        return sweep(update, jnp.zeros((6, FRAMES), jnp.float32))

    def depth_sweep(motion):
        def update(carry, source, target, adjoint, geo):
            lin_u, lin_v = apply_pose(geo, spread(motion, source, target, adjoint))
            return carry.at[source].add(geo[3] * geo[5] * lin_u + geo[4] * geo[6] * lin_v)
        return sweep(update, jnp.zeros((FRAMES, PIX), jnp.float32))

    def reduced(motion):
        image = depth_sweep(motion) / curvature
        return pose_sweep(motion, image) + pose_regularizer * motion

    rhs = pose_sweep(None, base_step)
    solution = jnp.zeros_like(rhs)
    residual = rhs
    direction = rhs
    norm_now = jnp.sum(residual * residual)
    for step in range(ITERS):
        product = reduced(direction)
        alpha = norm_now / jnp.sum(direction * product)
        solution = solution + alpha * direction
        residual = residual - alpha * product
        norm_next = jnp.sum(residual * residual)
        direction = residual + (norm_next / norm_now) * direction
        norm_now = norm_next
    depth_step = base_step - depth_sweep(solution) / curvature
    return solution, depth_step
```

```python
import functools
import jax
import jax.numpy as jnp
from jax import lax
from jax.experimental import pallas as pl
from jax.experimental.pallas import tpu as pltpu
from jax.sharding import PartitionSpec as P

ROWS = 48
COLS = 64
RADIUS = 8
ITERS = 6
REG = 100.0
F32 = jnp.float32
BF16 = jnp.bfloat16
L = 128
WIN = 32
SLOT = 24
VMEM_LIMIT = 60 * 1024 * 1024
UPPER = [(i, j) for i in range(6) for j in range(i, 6) if (i, j) != (0, 1)]


def split(x):
    high = x.astype(BF16)
    return high, (x - high.astype(F32)).astype(BF16)


def iota(shape, dim):
    return lax.broadcasted_iota(jnp.int32, shape, dim)


def aggregate(dest_ref, flow_ref, weight_ref, mask_ref, own_ref, low_ref, high_ref):
    edges = dest_ref.shape[1]
    tiles = mask_ref.shape[1] // L
    own = own_ref.shape[1]
    side = low_ref.shape[1]
    rows = own + 2 * side
    pick = (iota((rows, edges), 0) == dest_ref[...]).astype(F32).astype(BF16)
    for tile in range(tiles):
        cols = slice(tile * L, (tile + 1) * L)
        live = mask_ref[:, cols].astype(F32)
        fields = []
        for comp in range(2):
            take = pl.ds(tile * 2 + comp, edges, stride=2 * tiles)
            conf = weight_ref[take, :] * live
            fields += [conf, conf * flow_ref[take, :]]
        high, low = split(jnp.concatenate(fields, axis=1))
        out = jnp.dot(pick, high, preferred_element_type=F32) + jnp.dot(
            pick, low, preferred_element_type=F32
        )
        for field in range(4):
            part = out[:, field * L : (field + 1) * L]
            own_ref[field, :, cols] = part[:own]
            low_ref[field, :, cols] = part[own : own + side]
            high_ref[field, :, cols] = part[own + side :]


def jac_sums(u, v, uu, vv, uv, ds, a, b):
    return [
        ds * a,
        ds * b,
        -ds * (u * a + v * b),
        -uv * a - vv * b,
        uu * a + uv * b,
        u * b - v * a,
    ]


def adj_t(rel, cor, vec):
    out = []
    for j in range(3):
        out.append(rel[j] * vec[0] + rel[3 + j] * vec[1] + rel[6 + j] * vec[2])
    for j in range(3):
        out.append(
            cor[j] * vec[0]
            + cor[3 + j] * vec[1]
            + cor[6 + j] * vec[2]
            + rel[j] * vec[3]
            + rel[3 + j] * vec[4]
            + rel[6 + j] * vec[5]
        )
    return out


def build(
    first_ref, pose_ref, own_ref, low_ref, high_ref, depth_ref, damp_ref,
    matrix_ref, zh_ref, zl_ref, base_ref, scale_ref,
    frame_ref, pair_ref, hacc, racc, hc, rc, adc, wide, depth3, damp3,
):
    f_dev, pix = depth_ref.shape
    tiles = pix // L
    half = f_dev // 2
    ox, oy, oz = pose_ref[0], pose_ref[1], pose_ref[2]
    zero = jnp.zeros_like(ox)
    cross = [[zero, -oz, oy], [oz, zero, -ox], [-oy, ox, zero]]
    sq = ox * ox + oy * oy + oz * oz
    c1 = 1.0 - sq / 6.0 + sq * sq / 120.0
    c2 = 0.5 - sq / 24.0 + sq * sq / 720.0
    for r in range(3):
        for c in range(3):
            square = cross[r][0] * cross[0][c] + cross[r][1] * cross[1][c] + cross[r][2] * cross[2][c]
            frame_ref[3 * r + c] = float(r == c) + c1 * cross[r][c] + c2 * square
        frame_ref[9 + r] = pose_ref[3 + r]
    for tile in range(tiles):
        depth3[tile] = depth_ref[:, tile * L : (tile + 1) * L]
        damp3[tile] = damp_ref[:, tile * L : (tile + 1) * L]
    hc[...] = jnp.zeros_like(hc)
    rc[...] = jnp.zeros_like(rc)
    adc[...] = jnp.zeros_like(adc)
    lane = iota((SLOT, L), 1)
    row = iota((SLOT, L), 0)
    row8 = iota((8, L), 0)

    for part in range(2):
        base = part * half
        win = slice(base, base + SLOT)
        if part == 0:
            pad = lambda x: jnp.concatenate([x, jnp.zeros((WIN - SLOT, L), F32)], axis=0)
        else:
            pad = lambda x: jnp.concatenate([jnp.zeros((WIN - SLOT, L), F32), x], axis=0)

        @pl.loop(0, half)
        def per_source(i):
            s = i + base
            here = [frame_ref[k, pl.ds(s + RADIUS, 1), :] for k in range(12)]
            there = [frame_ref[k, win, :] for k in range(12)]
            rel = [
                there[3 * r] * here[3 * c]
                + there[3 * r + 1] * here[3 * c + 1]
                + there[3 * r + 2] * here[3 * c + 2]
                for r in range(3)
                for c in range(3)
            ]
            tr = [
                there[9 + r]
                - (rel[3 * r] * here[9] + rel[3 * r + 1] * here[10] + rel[3 * r + 2] * here[11])
                for r in range(3)
            ]
            cor = []
            for c in range(3):
                cor.append(tr[1] * rel[6 + c] - tr[2] * rel[3 + c])
            for c in range(3):
                cor.append(tr[2] * rel[c] - tr[0] * rel[6 + c])
            for c in range(3):
                cor.append(tr[0] * rel[3 + c] - tr[1] * rel[c])
            at = lane == s + RADIUS
            for k in range(9):
                pair_ref[k] = rel[k]
                pair_ref[12 + k] = cor[k]
                adc[k, win, :] = jnp.where(at, rel[k], adc[k, win, :])
                adc[9 + k, win, :] = jnp.where(at, cor[k], adc[9 + k, win, :])
            for k in range(3):
                pair_ref[9 + k] = tr[k]
            hacc[...] = jnp.zeros_like(hacc)
            racc[...] = jnp.zeros_like(racc)
            if part == 0:
                slot = jnp.where(i == 0, 4, jnp.where(i <= 4, i - 1, 7 - i))
                shift = jnp.where(i > 4, i, 0)
                keep = row8 >= i
            else:
                slot = jnp.where(i <= 3, i, jnp.where(i == 7, 4, 6 - i))
                shift = jnp.where((i > 3) & (i < 7), i + 1, 0)
                keep = row8 <= i
            is_source = row == s + RADIUS - base

            def per_tile(tile):
                cols = slice(tile * L, (tile + 1) * L)
                fields = []
                for k in range(4):
                    src = high_ref if part == 0 else low_ref
                    got = src[k, pl.ds(pl.multiple_of(slot * 8, 8), 8), cols]
                    got = jnp.where(keep, pltpu.roll(got, shift, 0), 0.0)
                    if part == 0:
                        mine = own_ref[k, pl.ds(pl.multiple_of(s * SLOT + 8, 8), 16), cols]
                        fields.append(jnp.concatenate([got, mine], axis=0))
                    else:
                        mine = own_ref[k, pl.ds(pl.multiple_of(s * SLOT, 8), 16), cols]
                        fields.append(jnp.concatenate([mine, got], axis=0))
                wu, fu, wv, fv = fields
                pixel = first_ref[0] + tile * L + iota((1, L), 1)
                prow = pixel // COLS
                pcol = pixel - prow * COLS
                col = (pcol.astype(F32) - 0.5 * (COLS - 1)) / COLS
                rowc = (prow.astype(F32) - 0.5 * (ROWS - 1)) / COLS
                depth = depth3[tile, pl.ds(s, 1), :]
                m = [pair_ref[k] for k in range(21)]
                point = [
                    m[3 * k] * col + m[3 * k + 1] * rowc + m[3 * k + 2] + depth * m[9 + k]
                    for k in range(3)
                ]
                iz = 1.0 / point[2]
                u = point[0] * iz
                v = point[1] * iz
                ds = depth * iz
                su = iz * (m[9] - u * m[11])
                sv = iz * (m[10] - v * m[11])
                au = wu * su
                av = wv * sv
                gu = wu * (col - u) + fu
                gv = wv * (rowc - v) + fv
                curv = jnp.sum(au * su + av * sv, axis=0, keepdims=True) + damp3[tile, pl.ds(s, 1), :]
                grad = -jnp.sum(su * gu + sv * gv, axis=0, keepdims=True)
                bstep = grad / curv
                scale = 1.0 / jnp.sqrt(curv)
                base_ref[tile, pl.ds(s, 1), :] = bstep
                scale_ref[tile, pl.ds(s, 1), :] = scale
                uu = 1.0 + u * u
                vv = 1.0 + v * v
                uv = u * v
                e = jac_sums(u, v, uu, vv, uv, ds, au, av)
                back = adj_t(m[0:9], m[12:21], e)
                zcols = pl.ds(pl.multiple_of(s * pix + tile * L, L), L)
                for j in range(6):
                    total = -jnp.sum(back[j], axis=0, keepdims=True)
                    full = jnp.where(is_source, total, e[j]) * scale
                    high, low = split(pad(full))
                    zh_ref[j * WIN : (j + 1) * WIN, zcols] = high
                    zl_ref[j * WIN : (j + 1) * WIN, zcols] = low
                r = jac_sums(u, v, uu, vv, uv, ds, -gu - au * bstep, -gv - av * bstep)
                for j in range(6):
                    racc[j] += r[j]
                ju = [ds, None, -ds * u, -uv, uu, -v]
                jv = [None, ds, -ds * v, -vv, uv, u]
                wju = [None if x is None else wu * x for x in ju]
                wjv = [None if x is None else wv * x for x in jv]
                for n, (a, b) in enumerate(UPPER):
                    terms = []
                    if ju[a] is not None and ju[b] is not None:
                        terms.append(wju[a] * ju[b])
                    if jv[a] is not None and jv[b] is not None:
                        terms.append(wjv[a] * jv[b])
                    hacc[n] += terms[0] if len(terms) == 1 else terms[0] + terms[1]

            for tile in range(tiles):
                per_tile(tile)
            for n in range(len(UPPER)):
                hc[n, win, :] = jnp.where(at, jnp.sum(hacc[n], axis=1, keepdims=True), hc[n, win, :])
            for j in range(6):
                rc[j, win, :] = jnp.where(at, jnp.sum(racc[j], axis=1, keepdims=True), rc[j, win, :])

    def accumulate(s, carry):
        hh, hl = carry
        cols = pl.ds(pl.multiple_of(s * pix, L), pix)
        zh = zh_ref[:, cols]
        zl = zl_ref[:, cols]
        nt = (((1,), (1,)), ((), ()))
        return (
            hh + lax.dot_general(zh, zh, nt, preferred_element_type=F32),
            hl + lax.dot_general(zh, zl, nt, preferred_element_type=F32),
        )

    none = jnp.zeros((6 * WIN, 6 * WIN), F32)
    hh, hl = lax.fori_loop(0, f_dev, accumulate, (none, none))

    h = [[None] * 6 for _ in range(6)]
    for n, (a, b) in enumerate(UPPER):
        h[a][b] = hc[n]
        h[b][a] = h[a][b]
    rel = [adc[k] for k in range(9)]
    cor = [adc[9 + k] for k in range(9)]
    ad = [[None] * 6 for _ in range(6)]
    for i in range(3):
        for j in range(3):
            ad[i][j] = rel[3 * i + j]
            ad[i][3 + j] = cor[3 * i + j]
            ad[3 + i][3 + j] = rel[3 * i + j]
    lane = iota((WIN, L), 1)
    row = iota((WIN, L), 0)
    eye = row == lane

    def total(terms):
        out = None
        for x, y in terms:
            if x is None or y is None:
                continue
            out = x * y if out is None else out + x * y
        return out

    had = [[total([(h[i][k], ad[k][j]) for k in range(6)]) for j in range(6)] for i in range(6)]
    wide[...] = jnp.zeros_like(wide)
    matrix_ref[...] = jnp.zeros_like(matrix_ref)
    for i in range(6):
        rows = slice(i * WIN, (i + 1) * WIN)
        for j in range(6):
            cols = slice(j * WIN, (j + 1) * WIN)
            wide[rows, cols] = -had[i][j][:, :WIN]
            both = jnp.sum(total([(ad[k][i], had[k][j]) for k in range(6)]), axis=0, keepdims=True)
            if h[i][j] is not None:
                both = both + jnp.sum(h[i][j], axis=1, keepdims=True)
            diag = jnp.where(eye, both, 0.0)
            matrix_ref[rows, cols] = diag[:, :WIN]
    wide[: 6 * WIN, : 6 * WIN] = wide[: 6 * WIN, : 6 * WIN] - hl
    flipped = wide[...].T
    matrix_ref[: 6 * WIN, : 6 * WIN] = (
        matrix_ref[: 6 * WIN, : 6 * WIN] - hh + wide[: 6 * WIN, : 6 * WIN] + flipped[: 6 * WIN, : 6 * WIN]
    )
    r = [rc[j] for j in range(6)]
    back = adj_t(rel, cor, r)
    for j in range(6):
        here = jnp.sum(jnp.where(eye, jnp.sum(r[j], axis=1, keepdims=True), 0.0) - back[j], axis=0, keepdims=True)
        matrix_ref[6 * WIN : 6 * WIN + 1, j * WIN : (j + 1) * WIN] = here[:, :WIN]


def finish(me_ref, all_ref, zh_ref, zl_ref, base_ref, scale_ref, pose_ref, step_ref, flat, cols_ref, step3):
    count = all_ref.shape[0]
    f_dev, pix = step_ref.shape
    width = all_ref.shape[2]
    size = 6 * WIN
    shape = (count, width)
    frame = iota(shape, 1) % WIN
    window = iota(shape, 0)
    below = (frame < f_dev) & (window > 0)
    above = (frame >= WIN - f_dev) & (window < count - 1)
    own = (frame >= RADIUS) & (frame < RADIUS + f_dev)

    def settle(x):
        down = pltpu.roll(pltpu.roll(x, 1, 0), width - f_dev, 1)
        up = pltpu.roll(pltpu.roll(x, count - 1, 0), f_dev, 1)
        return x + jnp.where(below, down, 0.0) + jnp.where(above, up, 0.0)

    def dot(x, y):
        return jnp.sum(jnp.where(own, x * y, 0.0), keepdims=True)

    def product(x):
        flat[0:count, :] = x
        tall = flat[...].T
        for w in range(count):
            cols_ref[...] = jnp.broadcast_to(tall[:size, w : w + 1], (size, L))
            pieces = []
            for lt in range(width // L):
                pieces.append(
                    jnp.sum(all_ref[w, :size, lt * L : (lt + 1) * L] * cols_ref[...], axis=0, keepdims=True)
                )
            flat[w : w + 1, :] = jnp.concatenate(pieces, axis=1)
        return settle(flat[0:count, :]) + REG * x

    flat[...] = jnp.zeros_like(flat)
    for w in range(count):
        flat[w : w + 1, :] = all_ref[w, size : size + 1, :]
    residual = settle(flat[0:count, :])
    x = jnp.zeros_like(residual)
    direction = residual
    rr = dot(residual, residual)
    for _ in range(ITERS):
        image = product(direction)
        alpha = rr / dot(direction, image)
        x = x + alpha * direction
        residual = residual - alpha * image
        new = dot(residual, residual)
        direction = residual + (new / rr) * direction
        rr = new
    flat[0:count, :] = x
    mine = flat[pl.ds(me_ref[0], 1), :]
    pose_ref[...] = jnp.broadcast_to(mine, pose_ref.shape)
    cols_ref[...] = jnp.broadcast_to(mine, (L, width)).T[:size]

    @pl.loop(0, f_dev)
    def per_source(s):
        for tile in range(pix // L):
            zcols = pl.ds(pl.multiple_of(s * pix + tile * L, L), L)
            z = zh_ref[:, zcols].astype(F32) + zl_ref[:, zcols].astype(F32)
            image = jnp.sum(z * cols_ref[...], axis=0, keepdims=True)
            here = (tile, pl.ds(s, 1), slice(None))
            step3[here] = base_ref[here] - scale_ref[here] * image

    for tile in range(pix // L):
        step_ref[:, tile * L : (tile + 1) * L] = step3[tile]


def call(body, out, scratch, smem, count):
    vm = pl.BlockSpec(memory_space=pltpu.VMEM)
    sm = pl.BlockSpec(memory_space=pltpu.SMEM)
    return pl.pallas_call(
        body,
        out_shape=[jax.ShapeDtypeStruct(s, t) for s, t in out],
        in_specs=[sm] * smem + [vm] * count,
        out_specs=[vm] * len(out),
        scratch_shapes=scratch,
        compiler_params=pltpu.CompilerParams(vmem_limit_bytes=VMEM_LIMIT),
    )


def shift(block, axis, distance):
    devices = range(lax.axis_size(axis))
    route = [(i - distance, i) for i in devices if i - distance in devices]
    return lax.ppermute(block, axis, route)


def per_device(edge_frames, rotvec, trans, inv_depth, depth_damping, flow, weight, mask):
    f_dev, pix = inv_depth.shape
    edges = mask.shape[0]
    tiles = pix // L
    me = lax.axis_index("frames")
    start = me * f_dev
    source = edge_frames[0] - start + RADIUS
    target = edge_frames[1] - start + RADIUS
    own_rows = f_dev * SLOT
    side = 40
    s = source - RADIUS
    mine = s * SLOT + target - (s // 8) * 8
    i = source
    q = target - 8
    tile = jnp.where(i <= 3, i, jnp.where(i == 7, 4, 6 - i))
    line = jnp.where((i > 3) & (i < 7), q + 7 - i, q)
    lowest = own_rows + tile * 8 + line
    i = source - f_dev - RADIUS
    q = target - f_dev
    tile = jnp.where(i == 0, 4, jnp.where(i <= 4, i - 1, 7 - i))
    line = jnp.where(i > 4, q - i, q)
    highest = own_rows + side + tile * 8 + line
    dest = jnp.where(source < RADIUS, lowest, jnp.where(source >= RADIUS + f_dev, highest, mine))

    def flat(x):
        return x.reshape(edges, 2, tiles, L).transpose(0, 2, 1, 3).reshape(edges * 2 * tiles, L)

    own, low, high = call(
        aggregate,
        [((4, own_rows, pix), F32), ((4, side, pix), F32), ((4, side, pix), F32)],
        [], 0, 4,
    )(dest.reshape(1, edges), flat(flow), flat(weight), mask)
    low = shift(low, "frames", -1)
    high = shift(high, "frames", 1)
    pose = jnp.pad(jnp.concatenate([rotvec, trans], axis=0), ((0, 0), (RADIUS, RADIUS)))
    pose = lax.dynamic_slice_in_dim(pose, start, WIN, axis=1)
    pose = jnp.broadcast_to(pose[:, :, None], (6, WIN, L))
    first = (lax.axis_index("pix") * pix).reshape(1).astype(jnp.int32)
    n = len(UPPER)
    width = 256
    matrix, zh, zl, base, scale = call(
        build,
        [
            ((6 * WIN + 8, width), F32),
            ((6 * WIN, f_dev * pix), BF16),
            ((6 * WIN, f_dev * pix), BF16),
            ((tiles, f_dev, L), F32),
            ((tiles, f_dev, L), F32),
        ],
        [
            pltpu.VMEM((12, WIN, L), F32),
            pltpu.VMEM((21, SLOT, L), F32),
            pltpu.VMEM((n, SLOT, L), F32),
            pltpu.VMEM((6, SLOT, L), F32),
            pltpu.VMEM((n, WIN, L), F32),
            pltpu.VMEM((6, WIN, L), F32),
            pltpu.VMEM((18, WIN, L), F32),
            pltpu.VMEM((256, 256), F32),
            pltpu.VMEM((tiles, f_dev, L), F32),
            pltpu.VMEM((tiles, f_dev, L), F32),
        ],
        1, 6,
    )(first, pose, own, low, high, inv_depth, depth_damping)
    matrix = lax.all_gather(lax.psum(matrix, "pix"), "frames")
    count = lax.axis_size("frames")
    x, step = call(
        finish,
        [((8, width), F32), ((f_dev, pix), F32)],
        [pltpu.VMEM((L, width), F32), pltpu.VMEM((6 * WIN, L), F32), pltpu.VMEM((tiles, f_dev, L), F32)],
        1, 5,
    )(me.reshape(1).astype(jnp.int32), matrix, zh, zl, base, scale)
    return (x[0].reshape(8, WIN)[:6, RADIUS : RADIUS + f_dev], step)


def solution(mesh):
    return jax.shard_map(
        per_device,
        mesh=mesh,
        in_specs=(
            P(None, "frames"),
            P(),
            P(),
            P("frames", "pix"),
            P("frames", "pix"),
            P("frames", None, "pix"),
            P("frames", None, "pix"),
            P("frames", "pix"),
        ),
        out_specs=(P(None, "frames"), P("frames", "pix")),
        check_vma=False,
    )
```

```python
import functools
import jax
import jax.numpy as jnp
from jax import lax
from jax.experimental import pallas as pl
from jax.experimental.pallas import tpu as pltpu
from jax.sharding import PartitionSpec as P

ROWS = 48
COLS = 64
RADIUS = 8
ITERS = 6
REG = 100.0
F32 = jnp.float32
BF16 = jnp.bfloat16
L = 128
WIN = 32
SLOT = 24
VMEM_LIMIT = 60 * 1024 * 1024
UPPER = [(i, j) for i in range(6) for j in range(i, 6) if (i, j) != (0, 1)]


def split(x):
    high = x.astype(BF16)
    return high, (x - high.astype(F32)).astype(BF16)


def iota(shape, dim):
    return lax.broadcasted_iota(jnp.int32, shape, dim)


def aggregate(dest_ref, flow_ref, weight_ref, mask_ref, own_ref, low_ref, high_ref):
    edges = dest_ref.shape[1]
    tiles = mask_ref.shape[1] // L
    own = own_ref.shape[1]
    side = low_ref.shape[1]
    rows = own + 2 * side
    pick = (iota((rows, edges), 0) == dest_ref[...]).astype(F32).astype(BF16)
    for tile in range(tiles):
        cols = slice(tile * L, (tile + 1) * L)
        live = mask_ref[:, cols].astype(F32)
        fields = []
        for comp in range(2):
            take = pl.ds(tile * 2 + comp, edges, stride=2 * tiles)
            conf = weight_ref[take, :] * live
            fields += [conf, conf * flow_ref[take, :]]
        high, low = split(jnp.concatenate(fields, axis=1))
        out = jnp.dot(pick, high, preferred_element_type=F32) + jnp.dot(
            pick, low, preferred_element_type=F32
        )
        for field in range(4):
            part = out[:, field * L : (field + 1) * L]
            own_ref[field, :, cols] = part[:own]
            low_ref[field, :, cols] = part[own : own + side]
            high_ref[field, :, cols] = part[own + side :]


def jac_sums(u, v, uu, vv, uv, ds, a, b):
    return [
        ds * a,
        ds * b,
        -ds * (u * a + v * b),
        -uv * a - vv * b,
        uu * a + uv * b,
        u * b - v * a,
    ]


def adj_t(rel, cor, vec):
    out = []
    for j in range(3):
        out.append(rel[j] * vec[0] + rel[3 + j] * vec[1] + rel[6 + j] * vec[2])
    for j in range(3):
        out.append(
            cor[j] * vec[0]
            + cor[3 + j] * vec[1]
            + cor[6 + j] * vec[2]
            + rel[j] * vec[3]
            + rel[3 + j] * vec[4]
            + rel[6 + j] * vec[5]
        )
    return out


def build(
    first_ref, pose_ref, own_ref, low_ref, high_ref, depth_ref, damp_ref,
    matrix_ref, zh_ref, zl_ref, base_ref, scale_ref,
    frame_ref, pair_ref, hacc, racc, hc, rc, adc, wide, depth3, damp3,
):
    f_dev, pix = depth_ref.shape
    tiles = pix // L
    half = f_dev // 2
    ox, oy, oz = pose_ref[0], pose_ref[1], pose_ref[2]
    zero = jnp.zeros_like(ox)
    cross = [[zero, -oz, oy], [oz, zero, -ox], [-oy, ox, zero]]
    sq = ox * ox + oy * oy + oz * oz
    c1 = 1.0 - sq / 6.0 + sq * sq / 120.0
    c2 = 0.5 - sq / 24.0 + sq * sq / 720.0
    for r in range(3):
        for c in range(3):
            square = cross[r][0] * cross[0][c] + cross[r][1] * cross[1][c] + cross[r][2] * cross[2][c]
            frame_ref[3 * r + c] = float(r == c) + c1 * cross[r][c] + c2 * square
        frame_ref[9 + r] = pose_ref[3 + r]
    for tile in range(tiles):
        depth3[tile] = depth_ref[:, tile * L : (tile + 1) * L]
        damp3[tile] = damp_ref[:, tile * L : (tile + 1) * L]
    hc[...] = jnp.zeros_like(hc)
    rc[...] = jnp.zeros_like(rc)
    adc[...] = jnp.zeros_like(adc)
    lane = iota((SLOT, L), 1)
    row = iota((SLOT, L), 0)
    row8 = iota((8, L), 0)

    for part in range(2):
        base = part * half
        win = slice(base, base + SLOT)
        if part == 0:
            pad = lambda x: jnp.concatenate([x, jnp.zeros((WIN - SLOT, L), F32)], axis=0)
        else:
            pad = lambda x: jnp.concatenate([jnp.zeros((WIN - SLOT, L), F32), x], axis=0)

        @pl.loop(0, half)
        def per_source(i):
            s = i + base
            here = [frame_ref[k, pl.ds(s + RADIUS, 1), :] for k in range(12)]
            there = [frame_ref[k, win, :] for k in range(12)]
            rel = [
                there[3 * r] * here[3 * c]
                + there[3 * r + 1] * here[3 * c + 1]
                + there[3 * r + 2] * here[3 * c + 2]
                for r in range(3)
                for c in range(3)
            ]
            tr = [
                there[9 + r]
                - (rel[3 * r] * here[9] + rel[3 * r + 1] * here[10] + rel[3 * r + 2] * here[11])
                for r in range(3)
            ]
            cor = []
            for c in range(3):
                cor.append(tr[1] * rel[6 + c] - tr[2] * rel[3 + c])
            for c in range(3):
                cor.append(tr[2] * rel[c] - tr[0] * rel[6 + c])
            for c in range(3):
                cor.append(tr[0] * rel[3 + c] - tr[1] * rel[c])
            at = lane == s + RADIUS
            for k in range(9):
                pair_ref[k] = rel[k]
                pair_ref[12 + k] = cor[k]
                adc[k, win, :] = jnp.where(at, rel[k], adc[k, win, :])
                adc[9 + k, win, :] = jnp.where(at, cor[k], adc[9 + k, win, :])
            for k in range(3):
                pair_ref[9 + k] = tr[k]
            hacc[...] = jnp.zeros_like(hacc)
            racc[...] = jnp.zeros_like(racc)
            if part == 0:
                slot = jnp.where(i == 0, 4, jnp.where(i <= 4, i - 1, 7 - i))
                shift = jnp.where(i > 4, i, 0)
                keep = row8 >= i
            else:
                slot = jnp.where(i <= 3, i, jnp.where(i == 7, 4, 6 - i))
                shift = jnp.where((i > 3) & (i < 7), i + 1, 0)
                keep = row8 <= i
            is_source = row == s + RADIUS - base

            def per_tile(tile):
                cols = slice(tile * L, (tile + 1) * L)
                fields = []
                for k in range(4):
                    src = high_ref if part == 0 else low_ref
                    got = src[k, pl.ds(pl.multiple_of(slot * 8, 8), 8), cols]
                    got = jnp.where(keep, pltpu.roll(got, shift, 0), 0.0)
                    if part == 0:
                        mine = own_ref[k, pl.ds(pl.multiple_of(s * SLOT + 8, 8), 16), cols]
                        fields.append(jnp.concatenate([got, mine], axis=0))
                    else:
                        mine = own_ref[k, pl.ds(pl.multiple_of(s * SLOT, 8), 16), cols]
                        fields.append(jnp.concatenate([mine, got], axis=0))
                wu, fu, wv, fv = fields
                pixel = first_ref[0] + tile * L + iota((1, L), 1)
                prow = pixel // COLS
                pcol = pixel - prow * COLS
                col = (pcol.astype(F32) - 0.5 * (COLS - 1)) / COLS
                rowc = (prow.astype(F32) - 0.5 * (ROWS - 1)) / COLS
                depth = depth3[tile, pl.ds(s, 1), :]
                m = [pair_ref[k] for k in range(21)]
                point = [
                    m[3 * k] * col + m[3 * k + 1] * rowc + m[3 * k + 2] + depth * m[9 + k]
                    for k in range(3)
                ]
                iz = 1.0 / point[2]
                u = point[0] * iz
                v = point[1] * iz
                ds = depth * iz
                su = iz * (m[9] - u * m[11])
                sv = iz * (m[10] - v * m[11])
                au = wu * su
                av = wv * sv
                gu = wu * (col - u) + fu
                gv = wv * (rowc - v) + fv
                curv = jnp.sum(au * su + av * sv, axis=0, keepdims=True) + damp3[tile, pl.ds(s, 1), :]
                grad = -jnp.sum(su * gu + sv * gv, axis=0, keepdims=True)
                bstep = grad / curv
                scale = 1.0 / jnp.sqrt(curv)
                base_ref[tile, pl.ds(s, 1), :] = bstep
                scale_ref[tile, pl.ds(s, 1), :] = scale
                uu = 1.0 + u * u
                vv = 1.0 + v * v
                uv = u * v
                e = jac_sums(u, v, uu, vv, uv, ds, au, av)
                back = adj_t(m[0:9], m[12:21], e)
                zcols = pl.ds(pl.multiple_of(s * pix + tile * L, L), L)
                for j in range(6):
                    total = -jnp.sum(back[j], axis=0, keepdims=True)
                    full = jnp.where(is_source, total, e[j]) * scale
                    high, low = split(pad(full))
                    zh_ref[j * WIN : (j + 1) * WIN, zcols] = high
                    zl_ref[j * WIN : (j + 1) * WIN, zcols] = low
                r = jac_sums(u, v, uu, vv, uv, ds, -gu - au * bstep, -gv - av * bstep)
                for j in range(6):
                    racc[j] += r[j]
                ju = [ds, None, -ds * u, -uv, uu, -v]
                jv = [None, ds, -ds * v, -vv, uv, u]
                wju = [None if x is None else wu * x for x in ju]
                wjv = [None if x is None else wv * x for x in jv]
                for n, (a, b) in enumerate(UPPER):
                    terms = []
                    if ju[a] is not None and ju[b] is not None:
                        terms.append(wju[a] * ju[b])
                    if jv[a] is not None and jv[b] is not None:
                        terms.append(wjv[a] * jv[b])
                    hacc[n] += terms[0] if len(terms) == 1 else terms[0] + terms[1]

            for tile in range(tiles):
                per_tile(tile)
            for n in range(len(UPPER)):
                hc[n, win, :] = jnp.where(at, jnp.sum(hacc[n], axis=1, keepdims=True), hc[n, win, :])
            for j in range(6):
                rc[j, win, :] = jnp.where(at, jnp.sum(racc[j], axis=1, keepdims=True), rc[j, win, :])

    def accumulate(s, carry):
        hh, hl = carry
        cols = pl.ds(pl.multiple_of(s * pix, L), pix)
        zh = zh_ref[:, cols]
        zl = zl_ref[:, cols]
        nt = (((1,), (1,)), ((), ()))
        return (
            hh + lax.dot_general(zh, zh, nt, preferred_element_type=F32),
            hl + lax.dot_general(zh, zl, nt, preferred_element_type=F32),
        )

    none = jnp.zeros((6 * WIN, 6 * WIN), F32)
    hh, hl = lax.fori_loop(0, f_dev, accumulate, (none, none))

    h = [[None] * 6 for _ in range(6)]
    for n, (a, b) in enumerate(UPPER):
        h[a][b] = hc[n]
        h[b][a] = h[a][b]
    rel = [adc[k] for k in range(9)]
    cor = [adc[9 + k] for k in range(9)]
    ad = [[None] * 6 for _ in range(6)]
    for i in range(3):
        for j in range(3):
            ad[i][j] = rel[3 * i + j]
            ad[i][3 + j] = cor[3 * i + j]
            ad[3 + i][3 + j] = rel[3 * i + j]
    lane = iota((WIN, L), 1)
    row = iota((WIN, L), 0)
    eye = row == lane

    def total(terms):
        out = None
        for x, y in terms:
            if x is None or y is None:
                continue
            out = x * y if out is None else out + x * y
        return out

    had = [[total([(h[i][k], ad[k][j]) for k in range(6)]) for j in range(6)] for i in range(6)]
    wide[...] = jnp.zeros_like(wide)
    matrix_ref[...] = jnp.zeros_like(matrix_ref)
    for i in range(6):
        rows = slice(i * WIN, (i + 1) * WIN)
        for j in range(6):
            cols = slice(j * WIN, (j + 1) * WIN)
            wide[rows, cols] = -had[i][j][:, :WIN]
            both = jnp.sum(total([(ad[k][i], had[k][j]) for k in range(6)]), axis=0, keepdims=True)
            if h[i][j] is not None:
                both = both + jnp.sum(h[i][j], axis=1, keepdims=True)
            diag = jnp.where(eye, both, 0.0)
            matrix_ref[rows, cols] = diag[:, :WIN]
    wide[: 6 * WIN, : 6 * WIN] = wide[: 6 * WIN, : 6 * WIN] - hl
    flipped = wide[...].T
    matrix_ref[: 6 * WIN, : 6 * WIN] = (
        matrix_ref[: 6 * WIN, : 6 * WIN] - hh + wide[: 6 * WIN, : 6 * WIN] + flipped[: 6 * WIN, : 6 * WIN]
    )
    r = [rc[j] for j in range(6)]
    back = adj_t(rel, cor, r)
    for j in range(6):
        here = jnp.sum(jnp.where(eye, jnp.sum(r[j], axis=1, keepdims=True), 0.0) - back[j], axis=0, keepdims=True)
        matrix_ref[6 * WIN : 6 * WIN + 1, j * WIN : (j + 1) * WIN] = here[:, :WIN]


def remote(src, dst, sems, phase, which, axis, peer):
    return pltpu.make_async_remote_copy(
        src_ref=src,
        dst_ref=dst,
        send_sem=sems.at[0, phase, which],
        recv_sem=sems.at[1, phase, which],
        device_id={axis: peer},
        device_id_type=pl.DeviceIdType.MESH,
    )


def peers(axis):
    count = lax.axis_size(axis)
    me = lax.axis_index(axis)
    return [lax.rem(me + step, count) for step in range(1, count)]


def finish(
    matrix_ref, zh_ref, zl_ref, base_ref, scale_ref, pose_ref, step_ref,
    flat, cols_ref, step3, land, summed, rows_ref, pix_sem, round_sem,
):
    count = lax.axis_size("frames")
    me = lax.axis_index("frames")
    f_dev, pix = step_ref.shape
    width = matrix_ref.shape[1]
    size = 6 * WIN
    zcount = lax.axis_size("pix")
    z = lax.axis_index("pix")
    chunk = matrix_ref.shape[0] // zcount

    def piece(which):
        return pl.ds(pl.multiple_of(which * chunk, 8), chunk)

    sent = []
    for peer in peers("pix"):
        copy = remote(matrix_ref.at[piece(peer)], land.at[z], pix_sem, 0, len(sent), "pix", peer)
        copy.start()
        sent.append(copy)
    land[z] = matrix_ref[piece(z), :]
    for copy in sent:
        copy.wait_recv()
    reduced = land[0]
    for k in range(1, zcount):
        reduced = reduced + land[k]
    for copy in sent:
        copy.wait_send()
    summed[piece(z), :] = reduced
    sent = []
    for peer in peers("pix"):
        copy = remote(summed.at[piece(z)], summed.at[piece(z)], pix_sem, 1, len(sent), "pix", peer)
        copy.start()
        sent.append(copy)
    for copy in sent:
        copy.wait_recv()
    for copy in sent:
        copy.wait_send()

    shape = (count, width)
    frame = iota(shape, 1) % WIN
    window = iota(shape, 0)
    below = (frame < f_dev) & (window > 0)
    above = (frame >= WIN - f_dev) & (window < count - 1)
    own = (frame >= RADIUS) & (frame < RADIUS + f_dev)

    def settle(x):
        down = pltpu.roll(pltpu.roll(x, 1, 0), width - f_dev, 1)
        up = pltpu.roll(pltpu.roll(x, count - 1, 0), f_dev, 1)
        return x + jnp.where(below, down, 0.0) + jnp.where(above, up, 0.0)

    def dot(x, y):
        return jnp.sum(jnp.where(own, x * y, 0.0), keepdims=True)

    def gather(step, row):
        rows_ref[step, me] = row
        sent = []
        here = rows_ref.at[step, me]
        for peer in peers("frames"):
            copy = remote(here, here, round_sem, step, len(sent), "frames", peer)
            copy.start()
            sent.append(copy)
        for copy in sent:
            copy.wait_recv()
        for w in range(count):
            flat[w : w + 1, :] = rows_ref[step, w]
        for copy in sent:
            copy.wait_send()
        return settle(flat[0:count, :])

    def product(step, x):
        flat[0:count, :] = x
        cols_ref[...] = jnp.broadcast_to(flat[pl.ds(me, 1), :], (L, width)).T[:size]
        pieces = []
        for lt in range(width // L):
            pieces.append(
                jnp.sum(summed[:size, lt * L : (lt + 1) * L] * cols_ref[...], axis=0, keepdims=True)
            )
        return gather(step, jnp.concatenate(pieces, axis=1)) + REG * x

    residual = gather(0, summed[size : size + 1, :])
    x = jnp.zeros_like(residual)
    direction = residual
    rr = dot(residual, residual)
    for step in range(ITERS):
        image = product(step + 1, direction)
        alpha = rr / dot(direction, image)
        x = x + alpha * direction
        residual = residual - alpha * image
        new = dot(residual, residual)
        direction = residual + (new / rr) * direction
        rr = new
    flat[0:count, :] = x
    mine = flat[pl.ds(me, 1), :]
    pose_ref[...] = jnp.broadcast_to(mine, pose_ref.shape)
    cols_ref[...] = jnp.broadcast_to(mine, (L, width)).T[:size]

    @pl.loop(0, f_dev)
    def per_source(s):
        for tile in range(pix // L):
            zcols = pl.ds(pl.multiple_of(s * pix + tile * L, L), L)
            z = zh_ref[:, zcols].astype(F32) + zl_ref[:, zcols].astype(F32)
            image = jnp.sum(z * cols_ref[...], axis=0, keepdims=True)
            here = (tile, pl.ds(s, 1), slice(None))
            step3[here] = base_ref[here] - scale_ref[here] * image

    for tile in range(pix // L):
        step_ref[:, tile * L : (tile + 1) * L] = step3[tile]


def solve(first_ref, pose_ref, own_ref, low_ref, high_ref, depth_ref, damp_ref, x_ref, step_ref, *scratch):
    matrix, zh, zl, base, scale = scratch[:5]
    barrier = pltpu.get_barrier_semaphore()
    total = 0
    for axis in ("frames", "pix"):
        for peer in peers(axis):
            pl.semaphore_signal(
                barrier, inc=1, device_id={axis: peer}, device_id_type=pl.DeviceIdType.MESH
            )
            total += 1
    build(
        first_ref, pose_ref, own_ref, low_ref, high_ref, depth_ref, damp_ref,
        matrix, zh, zl, base, scale, *scratch[5:15],
    )
    pl.semaphore_wait(barrier, total)
    finish(matrix, zh, zl, base, scale, x_ref, step_ref, *scratch[15:])


def call(body, out, scratch, smem, count, **params):
    vm = pl.BlockSpec(memory_space=pltpu.VMEM)
    sm = pl.BlockSpec(memory_space=pltpu.SMEM)
    return pl.pallas_call(
        body,
        out_shape=[jax.ShapeDtypeStruct(s, t) for s, t in out],
        in_specs=[sm] * smem + [vm] * count,
        out_specs=[vm] * len(out),
        scratch_shapes=scratch,
        compiler_params=pltpu.CompilerParams(vmem_limit_bytes=VMEM_LIMIT, **params),
    )


def shift(block, axis, distance):
    devices = range(lax.axis_size(axis))
    route = [(i - distance, i) for i in devices if i - distance in devices]
    return lax.ppermute(block, axis, route)


def per_device(edge_frames, rotvec, trans, inv_depth, depth_damping, flow, weight, mask):
    f_dev, pix = inv_depth.shape
    edges = mask.shape[0]
    tiles = pix // L
    me = lax.axis_index("frames")
    start = me * f_dev
    source = edge_frames[0] - start + RADIUS
    target = edge_frames[1] - start + RADIUS
    own_rows = f_dev * SLOT
    side = 40
    s = source - RADIUS
    mine = s * SLOT + target - (s // 8) * 8
    i = source
    q = target - 8
    tile = jnp.where(i <= 3, i, jnp.where(i == 7, 4, 6 - i))
    line = jnp.where((i > 3) & (i < 7), q + 7 - i, q)
    lowest = own_rows + tile * 8 + line
    i = source - f_dev - RADIUS
    q = target - f_dev
    tile = jnp.where(i == 0, 4, jnp.where(i <= 4, i - 1, 7 - i))
    line = jnp.where(i > 4, q - i, q)
    highest = own_rows + side + tile * 8 + line
    dest = jnp.where(source < RADIUS, lowest, jnp.where(source >= RADIUS + f_dev, highest, mine))

    def flat(x):
        return x.reshape(edges, 2, tiles, L).transpose(0, 2, 1, 3).reshape(edges * 2 * tiles, L)

    own, low, high = call(
        aggregate,
        [((4, own_rows, pix), F32), ((4, side, pix), F32), ((4, side, pix), F32)],
        [], 0, 4,
    )(dest.reshape(1, edges), flat(flow), flat(weight), mask)
    low = shift(low, "frames", -1)
    high = shift(high, "frames", 1)
    pose = jnp.pad(jnp.concatenate([rotvec, trans], axis=0), ((0, 0), (RADIUS, RADIUS)))
    pose = lax.dynamic_slice_in_dim(pose, start, WIN, axis=1)
    pose = jnp.broadcast_to(pose[:, :, None], (6, WIN, L))
    first = (lax.axis_index("pix") * pix).reshape(1).astype(jnp.int32)
    n = len(UPPER)
    width = 256
    count = lax.axis_size("frames")
    zcount = lax.axis_size("pix")
    chunk = -(-(6 * WIN + 8) // (8 * zcount)) * 8
    x, step = call(
        solve,
        [((8, width), F32), ((f_dev, pix), F32)],
        [
            pltpu.VMEM((chunk * zcount, width), F32),
            pltpu.VMEM((6 * WIN, f_dev * pix), BF16),
            pltpu.VMEM((6 * WIN, f_dev * pix), BF16),
            pltpu.VMEM((tiles, f_dev, L), F32),
            pltpu.VMEM((tiles, f_dev, L), F32),
            pltpu.VMEM((12, WIN, L), F32),
            pltpu.VMEM((21, SLOT, L), F32),
            pltpu.VMEM((n, SLOT, L), F32),
            pltpu.VMEM((6, SLOT, L), F32),
            pltpu.VMEM((n, WIN, L), F32),
            pltpu.VMEM((6, WIN, L), F32),
            pltpu.VMEM((18, WIN, L), F32),
            pltpu.VMEM((256, 256), F32),
            pltpu.VMEM((tiles, f_dev, L), F32),
            pltpu.VMEM((tiles, f_dev, L), F32),
            pltpu.VMEM((L, width), F32),
            pltpu.VMEM((6 * WIN, L), F32),
            pltpu.VMEM((tiles, f_dev, L), F32),
            pltpu.VMEM((zcount, chunk, width), F32),
            pltpu.VMEM((chunk * zcount, width), F32),
            pltpu.VMEM((ITERS + 1, count, 1, width), F32),
            pltpu.SemaphoreType.DMA((2, 2, zcount)),
            pltpu.SemaphoreType.DMA((2, ITERS + 1, count)),
        ],
        1, 6, collective_id=0, has_side_effects=True,
    )(first, pose, own, low, high, inv_depth, depth_damping)
    return (x[0].reshape(8, WIN)[:6, RADIUS : RADIUS + f_dev], step)


def solution(mesh):
    return jax.shard_map(
        per_device,
        mesh=mesh,
        in_specs=(
            P(None, "frames"),
            P(),
            P(),
            P("frames", "pix"),
            P("frames", "pix"),
            P("frames", None, "pix"),
            P("frames", None, "pix"),
            P("frames", "pix"),
        ),
        out_specs=(P(None, "frames"), P("frames", "pix")),
        check_vma=False,
    )
```

```python
import functools
import jax
import jax.numpy as jnp
from jax import lax
from jax.experimental import pallas as pl
from jax.experimental.pallas import tpu as pltpu
from jax.sharding import PartitionSpec as P

ROWS = 48
COLS = 64
RADIUS = 8
ITERS = 6
REG = 100.0
F32 = jnp.float32
BF16 = jnp.bfloat16
L = 128
WIN = 32
SLOT = 24
VMEM_LIMIT = 60 * 1024 * 1024
UPPER = [(i, j) for i in range(6) for j in range(i, 6) if (i, j) != (0, 1)]


def split(x):
    high = x.astype(BF16)
    return high, (x - high.astype(F32)).astype(BF16)


def iota(shape, dim):
    return lax.broadcasted_iota(jnp.int32, shape, dim)


def aggregate(dest_ref, flow_ref, weight_ref, mask_ref, own_ref, low_ref, high_ref):
    edges = dest_ref.shape[1]
    tiles = mask_ref.shape[1] // L
    own = own_ref.shape[1]
    side = low_ref.shape[1]
    rows = own + 2 * side
    pick = (iota((rows, edges), 0) == dest_ref[...]).astype(F32).astype(BF16)
    for tile in range(tiles):
        cols = slice(tile * L, (tile + 1) * L)
        live = mask_ref[:, cols].astype(F32)
        fields = []
        for comp in range(2):
            take = pl.ds(tile * 2 + comp, edges, stride=2 * tiles)
            conf = weight_ref[take, :] * live
            fields += [conf, conf * flow_ref[take, :]]
        high, low = split(jnp.concatenate(fields, axis=1))
        out = jnp.dot(pick, high, preferred_element_type=F32) + jnp.dot(
            pick, low, preferred_element_type=F32
        )
        for field in range(4):
            part = out[:, field * L : (field + 1) * L]
            own_ref[field, :, cols] = part[:own]
            low_ref[field, :, cols] = part[own : own + side]
            high_ref[field, :, cols] = part[own + side :]


def jac_sums(u, v, uu, vv, uv, ds, a, b):
    return [
        ds * a,
        ds * b,
        -ds * (u * a + v * b),
        -uv * a - vv * b,
        uu * a + uv * b,
        u * b - v * a,
    ]


def adj_t(rel, cor, vec):
    out = []
    for j in range(3):
        out.append(rel[j] * vec[0] + rel[3 + j] * vec[1] + rel[6 + j] * vec[2])
    for j in range(3):
        out.append(
            cor[j] * vec[0]
            + cor[3 + j] * vec[1]
            + cor[6 + j] * vec[2]
            + rel[j] * vec[3]
            + rel[3 + j] * vec[4]
            + rel[6 + j] * vec[5]
        )
    return out


def build(
    first_ref, pose_ref, own_ref, low_ref, high_ref, depth_ref, damp_ref,
    matrix_ref, zh_ref, zl_ref, base_ref, scale_ref,
    frame_ref, pair_ref, hacc, racc, hc, rc, adc, wide, depth3, damp3,
):
    f_dev, pix = depth_ref.shape
    tiles = pix // L
    half = f_dev // 2
    ox, oy, oz = pose_ref[0], pose_ref[1], pose_ref[2]
    zero = jnp.zeros_like(ox)
    cross = [[zero, -oz, oy], [oz, zero, -ox], [-oy, ox, zero]]
    sq = ox * ox + oy * oy + oz * oz
    c1 = 1.0 - sq / 6.0 + sq * sq / 120.0
    c2 = 0.5 - sq / 24.0 + sq * sq / 720.0
    for r in range(3):
        for c in range(3):
            square = cross[r][0] * cross[0][c] + cross[r][1] * cross[1][c] + cross[r][2] * cross[2][c]
            frame_ref[3 * r + c] = float(r == c) + c1 * cross[r][c] + c2 * square
        frame_ref[9 + r] = pose_ref[3 + r]
    for tile in range(tiles):
        depth3[tile] = depth_ref[:, tile * L : (tile + 1) * L]
        damp3[tile] = damp_ref[:, tile * L : (tile + 1) * L]
    hc[...] = jnp.zeros_like(hc)
    rc[...] = jnp.zeros_like(rc)
    adc[...] = jnp.zeros_like(adc)
    lane = iota((SLOT, L), 1)
    row = iota((SLOT, L), 0)
    row8 = iota((8, L), 0)

    for part in range(2):
        base = part * half
        win = slice(base, base + SLOT)
        if part == 0:
            pad = lambda x: jnp.concatenate([x, jnp.zeros((WIN - SLOT, L), F32)], axis=0)
        else:
            pad = lambda x: jnp.concatenate([jnp.zeros((WIN - SLOT, L), F32), x], axis=0)

        @pl.loop(0, half)
        def per_source(i):
            s = i + base
            here = [frame_ref[k, pl.ds(s + RADIUS, 1), :] for k in range(12)]
            there = [frame_ref[k, win, :] for k in range(12)]
            rel = [
                there[3 * r] * here[3 * c]
                + there[3 * r + 1] * here[3 * c + 1]
                + there[3 * r + 2] * here[3 * c + 2]
                for r in range(3)
                for c in range(3)
            ]
            tr = [
                there[9 + r]
                - (rel[3 * r] * here[9] + rel[3 * r + 1] * here[10] + rel[3 * r + 2] * here[11])
                for r in range(3)
            ]
            cor = []
            for c in range(3):
                cor.append(tr[1] * rel[6 + c] - tr[2] * rel[3 + c])
            for c in range(3):
                cor.append(tr[2] * rel[c] - tr[0] * rel[6 + c])
            for c in range(3):
                cor.append(tr[0] * rel[3 + c] - tr[1] * rel[c])
            at = lane == s + RADIUS
            for k in range(9):
                pair_ref[k] = rel[k]
                pair_ref[12 + k] = cor[k]
                adc[k, win, :] = jnp.where(at, rel[k], adc[k, win, :])
                adc[9 + k, win, :] = jnp.where(at, cor[k], adc[9 + k, win, :])
            for k in range(3):
                pair_ref[9 + k] = tr[k]
            hacc[...] = jnp.zeros_like(hacc)
            racc[...] = jnp.zeros_like(racc)
            if part == 0:
                slot = jnp.where(i == 0, 4, jnp.where(i <= 4, i - 1, 7 - i))
                shift = jnp.where(i > 4, i, 0)
                keep = row8 >= i
            else:
                slot = jnp.where(i <= 3, i, jnp.where(i == 7, 4, 6 - i))
                shift = jnp.where((i > 3) & (i < 7), i + 1, 0)
                keep = row8 <= i
            is_source = row == s + RADIUS - base

            def per_tile(tile):
                cols = slice(tile * L, (tile + 1) * L)
                fields = []
                for k in range(4):
                    src = high_ref if part == 0 else low_ref
                    got = src[k, pl.ds(pl.multiple_of(slot * 8, 8), 8), cols]
                    got = jnp.where(keep, pltpu.roll(got, shift, 0), 0.0)
                    if part == 0:
                        mine = own_ref[k, pl.ds(pl.multiple_of(s * SLOT + 8, 8), 16), cols]
                        fields.append(jnp.concatenate([got, mine], axis=0))
                    else:
                        mine = own_ref[k, pl.ds(pl.multiple_of(s * SLOT, 8), 16), cols]
                        fields.append(jnp.concatenate([mine, got], axis=0))
                wu, fu, wv, fv = fields
                pixel = first_ref[0] + tile * L + iota((1, L), 1)
                prow = pixel // COLS
                pcol = pixel - prow * COLS
                col = (pcol.astype(F32) - 0.5 * (COLS - 1)) / COLS
                rowc = (prow.astype(F32) - 0.5 * (ROWS - 1)) / COLS
                depth = depth3[tile, pl.ds(s, 1), :]
                m = [pair_ref[k] for k in range(21)]
                point = [
                    m[3 * k] * col + m[3 * k + 1] * rowc + m[3 * k + 2] + depth * m[9 + k]
                    for k in range(3)
                ]
                iz = 1.0 / point[2]
                u = point[0] * iz
                v = point[1] * iz
                ds = depth * iz
                su = iz * (m[9] - u * m[11])
                sv = iz * (m[10] - v * m[11])
                au = wu * su
                av = wv * sv
                gu = wu * (col - u) + fu
                gv = wv * (rowc - v) + fv
                curv = jnp.sum(au * su + av * sv, axis=0, keepdims=True) + damp3[tile, pl.ds(s, 1), :]
                grad = -jnp.sum(su * gu + sv * gv, axis=0, keepdims=True)
                bstep = grad / curv
                scale = 1.0 / jnp.sqrt(curv)
                base_ref[tile, pl.ds(s, 1), :] = bstep
                scale_ref[tile, pl.ds(s, 1), :] = scale
                uu = 1.0 + u * u
                vv = 1.0 + v * v
                uv = u * v
                e = jac_sums(u, v, uu, vv, uv, ds, au, av)
                back = adj_t(m[0:9], m[12:21], e)
                zcols = pl.ds(pl.multiple_of(s * pix + tile * L, L), L)
                for j in range(6):
                    total = -jnp.sum(back[j], axis=0, keepdims=True)
                    full = jnp.where(is_source, total, e[j]) * scale
                    high, low = split(pad(full))
                    zh_ref[j * WIN : (j + 1) * WIN, zcols] = high
                    zl_ref[j * WIN : (j + 1) * WIN, zcols] = low
                r = jac_sums(u, v, uu, vv, uv, ds, -gu - au * bstep, -gv - av * bstep)
                for j in range(6):
                    racc[j] += r[j]
                ju = [ds, None, -ds * u, -uv, uu, -v]
                jv = [None, ds, -ds * v, -vv, uv, u]
                wju = [None if x is None else wu * x for x in ju]
                wjv = [None if x is None else wv * x for x in jv]
                for n, (a, b) in enumerate(UPPER):
                    terms = []
                    if ju[a] is not None and ju[b] is not None:
                        terms.append(wju[a] * ju[b])
                    if jv[a] is not None and jv[b] is not None:
                        terms.append(wjv[a] * jv[b])
                    hacc[n] += terms[0] if len(terms) == 1 else terms[0] + terms[1]

            for tile in range(tiles):
                per_tile(tile)
            for n in range(len(UPPER)):
                hc[n, win, :] = jnp.where(at, jnp.sum(hacc[n], axis=1, keepdims=True), hc[n, win, :])
            for j in range(6):
                rc[j, win, :] = jnp.where(at, jnp.sum(racc[j], axis=1, keepdims=True), rc[j, win, :])

    def accumulate(s, carry):
        hh, hl = carry
        cols = pl.ds(pl.multiple_of(s * pix, L), pix)
        zh = zh_ref[:, cols]
        zl = zl_ref[:, cols]
        nt = (((1,), (1,)), ((), ()))
        return (
            hh + lax.dot_general(zh, zh, nt, preferred_element_type=F32),
            hl + lax.dot_general(zh, zl, nt, preferred_element_type=F32),
        )

    none = jnp.zeros((6 * WIN, 6 * WIN), F32)
    hh, hl = lax.fori_loop(0, f_dev, accumulate, (none, none))

    h = [[None] * 6 for _ in range(6)]
    for n, (a, b) in enumerate(UPPER):
        h[a][b] = hc[n]
        h[b][a] = h[a][b]
    rel = [adc[k] for k in range(9)]
    cor = [adc[9 + k] for k in range(9)]
    ad = [[None] * 6 for _ in range(6)]
    for i in range(3):
        for j in range(3):
            ad[i][j] = rel[3 * i + j]
            ad[i][3 + j] = cor[3 * i + j]
            ad[3 + i][3 + j] = rel[3 * i + j]
    lane = iota((WIN, L), 1)
    row = iota((WIN, L), 0)
    eye = row == lane

    def total(terms):
        out = None
        for x, y in terms:
            if x is None or y is None:
                continue
            out = x * y if out is None else out + x * y
        return out

    had = [[total([(h[i][k], ad[k][j]) for k in range(6)]) for j in range(6)] for i in range(6)]
    wide[...] = jnp.zeros_like(wide)
    matrix_ref[...] = jnp.zeros_like(matrix_ref)
    for i in range(6):
        rows = slice(i * WIN, (i + 1) * WIN)
        for j in range(6):
            cols = slice(j * WIN, (j + 1) * WIN)
            wide[rows, cols] = -had[i][j][:, :WIN]
            both = jnp.sum(total([(ad[k][i], had[k][j]) for k in range(6)]), axis=0, keepdims=True)
            if h[i][j] is not None:
                both = both + jnp.sum(h[i][j], axis=1, keepdims=True)
            diag = jnp.where(eye, both, 0.0)
            matrix_ref[rows, cols] = diag[:, :WIN]
    wide[: 6 * WIN, : 6 * WIN] = wide[: 6 * WIN, : 6 * WIN] - hl
    flipped = wide[...].T
    matrix_ref[: 6 * WIN, : 6 * WIN] = (
        matrix_ref[: 6 * WIN, : 6 * WIN] - hh + wide[: 6 * WIN, : 6 * WIN] + flipped[: 6 * WIN, : 6 * WIN]
    )
    r = [rc[j] for j in range(6)]
    back = adj_t(rel, cor, r)
    for j in range(6):
        here = jnp.sum(jnp.where(eye, jnp.sum(r[j], axis=1, keepdims=True), 0.0) - back[j], axis=0, keepdims=True)
        matrix_ref[6 * WIN : 6 * WIN + 1, j * WIN : (j + 1) * WIN] = here[:, :WIN]


def remote(src, dst, sems, phase, which, axis, peer):
    return pltpu.make_async_remote_copy(
        src_ref=src,
        dst_ref=dst,
        send_sem=sems.at[0, phase, which],
        recv_sem=sems.at[1, phase, which],
        device_id={axis: peer},
        device_id_type=pl.DeviceIdType.MESH,
    )


def peers(axis):
    count = lax.axis_size(axis)
    me = lax.axis_index(axis)
    return [lax.rem(me + step, count) for step in range(1, count)]


def finish(
    matrix_ref, zh_ref, zl_ref, base_ref, scale_ref, pose_ref, step_ref,
    flat, cols_ref, step3, land, summed, rows_ref, pix_sem, round_sem,
):
    count = lax.axis_size("frames")
    me = lax.axis_index("frames")
    f_dev, pix = step_ref.shape
    width = matrix_ref.shape[1]
    size = 6 * WIN
    zcount = lax.axis_size("pix")
    z = lax.axis_index("pix")
    chunk = matrix_ref.shape[0] // zcount

    def piece(which):
        return pl.ds(pl.multiple_of(which * chunk, 8), chunk)

    sent = []
    for peer in peers("pix"):
        copy = remote(matrix_ref.at[piece(peer)], land.at[z], pix_sem, 0, len(sent), "pix", peer)
        copy.start()
        sent.append(copy)
    land[z] = matrix_ref[piece(z), :]
    for copy in sent:
        copy.wait_recv()
    reduced = land[0]
    for k in range(1, zcount):
        reduced = reduced + land[k]
    for copy in sent:
        copy.wait_send()
    summed[piece(z), :] = reduced
    sent = []
    for peer in peers("pix"):
        copy = remote(summed.at[piece(z)], summed.at[piece(z)], pix_sem, 1, len(sent), "pix", peer)
        copy.start()
        sent.append(copy)
    for copy in sent:
        copy.wait_recv()
    for copy in sent:
        copy.wait_send()

    shape = (count, width)
    frame = iota(shape, 1) % WIN
    window = iota(shape, 0)
    below = (frame < f_dev) & (window > 0)
    above = (frame >= WIN - f_dev) & (window < count - 1)
    own = (frame >= RADIUS) & (frame < RADIUS + f_dev)

    def settle(x):
        down = pltpu.roll(pltpu.roll(x, 1, 0), width - f_dev, 1)
        up = pltpu.roll(pltpu.roll(x, count - 1, 0), f_dev, 1)
        return x + jnp.where(below, down, 0.0) + jnp.where(above, up, 0.0)

    def dot(x, y):
        return jnp.sum(jnp.where(own, x * y, 0.0), keepdims=True)

    def gather(step, row):
        rows_ref[step, me] = row
        sent = []
        here = rows_ref.at[step, me]
        for peer in peers("frames"):
            copy = remote(here, here, round_sem, step, len(sent), "frames", peer)
            copy.start()
            sent.append(copy)
        for copy in sent:
            copy.wait_recv()
        for w in range(count):
            flat[w : w + 1, :] = rows_ref[step, w]
        for copy in sent:
            copy.wait_send()
        return settle(flat[0:count, :])

    def product(step, x):
        flat[0:count, :] = x
        cols_ref[...] = jnp.broadcast_to(flat[pl.ds(me, 1), :], (L, width)).T[:size]
        pieces = []
        for lt in range(width // L):
            pieces.append(
                jnp.sum(summed[:size, lt * L : (lt + 1) * L] * cols_ref[...], axis=0, keepdims=True)
            )
        return gather(step, jnp.concatenate(pieces, axis=1)) + REG * x

    residual = gather(0, summed[size : size + 1, :])
    x = jnp.zeros_like(residual)
    direction = residual
    rr = dot(residual, residual)
    for step in range(ITERS):
        image = product(step + 1, direction)
        alpha = rr / dot(direction, image)
        x = x + alpha * direction
        residual = residual - alpha * image
        new = dot(residual, residual)
        direction = residual + (new / rr) * direction
        rr = new
    flat[0:count, :] = x
    mine = flat[pl.ds(me, 1), :]
    pose_ref[...] = jnp.broadcast_to(mine, pose_ref.shape)
    cols_ref[...] = jnp.broadcast_to(mine, (L, width)).T[:size]

    @pl.loop(0, f_dev)
    def per_source(s):
        for tile in range(pix // L):
            zcols = pl.ds(pl.multiple_of(s * pix + tile * L, L), L)
            z = zh_ref[:, zcols].astype(F32) + zl_ref[:, zcols].astype(F32)
            image = jnp.sum(z * cols_ref[...], axis=0, keepdims=True)
            here = (tile, pl.ds(s, 1), slice(None))
            step3[here] = base_ref[here] - scale_ref[here] * image

    for tile in range(pix // L):
        step_ref[:, tile * L : (tile + 1) * L] = step3[tile]


def solve(
    first_ref, dest_ref, flow_ref, weight_ref, mask_ref, pose_ref, depth_ref, damp_ref,
    x_ref, step_ref, own_ref, low_out, high_out, low_ref, high_ref, edge_sem, *scratch,
):
    matrix, zh, zl, base, scale = scratch[:5]
    barrier = pltpu.get_barrier_semaphore()
    total = 0
    for axis in ("frames", "pix"):
        for peer in peers(axis):
            pl.semaphore_signal(
                barrier, inc=1, device_id={axis: peer}, device_id_type=pl.DeviceIdType.MESH
            )
            total += 1
    aggregate(dest_ref, flow_ref, weight_ref, mask_ref, own_ref, low_out, high_out)
    pl.semaphore_wait(barrier, total)
    around = peers("frames")
    edge = [
        remote(low_out, low_ref, edge_sem, 0, 0, "frames", around[-1]),
        remote(high_out, high_ref, edge_sem, 1, 0, "frames", around[0]),
    ]
    for copy in edge:
        copy.start()
    for copy in edge:
        copy.wait()
    build(
        first_ref, pose_ref, own_ref, low_ref, high_ref, depth_ref, damp_ref,
        matrix, zh, zl, base, scale, *scratch[5:15],
    )
    finish(matrix, zh, zl, base, scale, x_ref, step_ref, *scratch[15:])


def call(body, out, scratch, smem, count, **params):
    vm = pl.BlockSpec(memory_space=pltpu.VMEM)
    sm = pl.BlockSpec(memory_space=pltpu.SMEM)
    return pl.pallas_call(
        body,
        out_shape=[jax.ShapeDtypeStruct(s, t) for s, t in out],
        in_specs=[sm] * smem + [vm] * count,
        out_specs=[vm] * len(out),
        scratch_shapes=scratch,
        compiler_params=pltpu.CompilerParams(vmem_limit_bytes=VMEM_LIMIT, **params),
    )


def per_device(edge_frames, rotvec, trans, inv_depth, depth_damping, flow, weight, mask):
    f_dev, pix = inv_depth.shape
    edges = mask.shape[0]
    tiles = pix // L
    me = lax.axis_index("frames")
    start = me * f_dev
    source = edge_frames[0] - start + RADIUS
    target = edge_frames[1] - start + RADIUS
    own_rows = f_dev * SLOT
    side = 40
    s = source - RADIUS
    mine = s * SLOT + target - (s // 8) * 8
    i = source
    q = target - 8
    tile = jnp.where(i <= 3, i, jnp.where(i == 7, 4, 6 - i))
    line = jnp.where((i > 3) & (i < 7), q + 7 - i, q)
    lowest = own_rows + tile * 8 + line
    i = source - f_dev - RADIUS
    q = target - f_dev
    tile = jnp.where(i == 0, 4, jnp.where(i <= 4, i - 1, 7 - i))
    line = jnp.where(i > 4, q - i, q)
    highest = own_rows + side + tile * 8 + line
    dest = jnp.where(source < RADIUS, lowest, jnp.where(source >= RADIUS + f_dev, highest, mine))

    def flat(x):
        return x.reshape(edges, 2, tiles, L).transpose(0, 2, 1, 3).reshape(edges * 2 * tiles, L)

    pose = jnp.pad(jnp.concatenate([rotvec, trans], axis=0), ((0, 0), (RADIUS, RADIUS)))
    pose = lax.dynamic_slice_in_dim(pose, start, WIN, axis=1)
    pose = jnp.broadcast_to(pose[:, :, None], (6, WIN, L))
    first = (lax.axis_index("pix") * pix).reshape(1).astype(jnp.int32)
    n = len(UPPER)
    width = 256
    count = lax.axis_size("frames")
    zcount = lax.axis_size("pix")
    chunk = -(-(6 * WIN + 8) // (8 * zcount)) * 8
    x, step = call(
        solve,
        [((8, width), F32), ((f_dev, pix), F32)],
        [
            pltpu.VMEM((4, own_rows, pix), F32),
            pltpu.VMEM((4, side, pix), F32),
            pltpu.VMEM((4, side, pix), F32),
            pltpu.VMEM((4, side, pix), F32),
            pltpu.VMEM((4, side, pix), F32),
            pltpu.SemaphoreType.DMA((2, 2, 1)),
            pltpu.VMEM((chunk * zcount, width), F32),
            pltpu.VMEM((6 * WIN, f_dev * pix), BF16),
            pltpu.VMEM((6 * WIN, f_dev * pix), BF16),
            pltpu.VMEM((tiles, f_dev, L), F32),
            pltpu.VMEM((tiles, f_dev, L), F32),
            pltpu.VMEM((12, WIN, L), F32),
            pltpu.VMEM((21, SLOT, L), F32),
            pltpu.VMEM((n, SLOT, L), F32),
            pltpu.VMEM((6, SLOT, L), F32),
            pltpu.VMEM((n, WIN, L), F32),
            pltpu.VMEM((6, WIN, L), F32),
            pltpu.VMEM((18, WIN, L), F32),
            pltpu.VMEM((256, 256), F32),
            pltpu.VMEM((tiles, f_dev, L), F32),
            pltpu.VMEM((tiles, f_dev, L), F32),
            pltpu.VMEM((L, width), F32),
            pltpu.VMEM((6 * WIN, L), F32),
            pltpu.VMEM((tiles, f_dev, L), F32),
            pltpu.VMEM((zcount, chunk, width), F32),
            pltpu.VMEM((chunk * zcount, width), F32),
            pltpu.VMEM((ITERS + 1, count, 1, width), F32),
            pltpu.SemaphoreType.DMA((2, 2, zcount)),
            pltpu.SemaphoreType.DMA((2, ITERS + 1, count)),
        ],
        1, 7, collective_id=0, has_side_effects=True,
    )(
        first, dest.reshape(1, edges), flat(flow), flat(weight), mask,
        pose, inv_depth, depth_damping,
    )
    return (x[0].reshape(8, WIN)[:6, RADIUS : RADIUS + f_dev], step)


def solution(mesh):
    return jax.shard_map(
        per_device,
        mesh=mesh,
        in_specs=(
            P(None, "frames"),
            P(),
            P(),
            P("frames", "pix"),
            P("frames", "pix"),
            P("frames", None, "pix"),
            P("frames", None, "pix"),
            P("frames", "pix"),
        ),
        out_specs=(P(None, "frames"), P("frames", "pix")),
        check_vma=False,
    )
```
